128 devices in a mesh: segment: 4 (over x_lo, core), fsdp: 8 (over z, x_hi), dp: 4 (over y).
Axes of the slice: x: 4 (x_hi: 2, x_lo: 2; x = x_hi * 2 + x_lo), y: 4, z: 4, core: 2. Of those that a mesh axis runs over, the one named last changes fastest.
Arguments:
- inputs: bfloat16 [3, 64, 49, 2880], P(None, ('fsdp', 'dp')), may hold values from -6 to 6
- cotangent: bfloat16 [3, 64, 49, 2880], P(None, ('fsdp', 'dp')), may hold values from -0.119628906 to 0.119628906
- plan: int32 [3], replicated, may hold values from 0 to 2, each once
- weight: bfloat16 [4, 2880, 2880], P('segment', 'fsdp'), may hold values from -0.109375 to 0.109375
- squeeze: bfloat16 [4, 2880, 360], P('segment', 'fsdp'), may hold values from -0.109375 to 0.109375
- excite: bfloat16 [4, 2880, 360], P('segment', 'fsdp'), may hold values from -0.3125 to 0.3125
Outputs:
- grad_weight: float32 [4, 2880, 2880], P('segment', ('fsdp', 'dp'))
- grad_squeeze: float32 [4, 2880, 360], P('segment', ('fsdp', 'dp'))
- grad_excite: float32 [4, 2880, 360], P('segment', ('fsdp', 'dp'))
The draws below stay inside these ranges and needn't reach their ends.
Inputs may be any that keep to these rules, and one draw needn't show every extreme that they name: plan names each of the 3 microbatches exactly once.
All inputs are finite; a program needn't handle non-finite values.
Results may differ from the reference program's by a relative error of at most 0.024.
Values may be sent and summed in bfloat16 or wider, within the bound.
A program may use at most 128 MiB of HBM per device.

```python
import jax
import jax.numpy as jnp
from jax import lax

C = 2880
R = 360
PIX = 49
MICRO = 3
IMG_DEV = 2
IMAGES = 64
SEGMENTS = 4
N_SEGMENT = 4


def block_levels(stream_key, dims, shards, least, top_value):
    def one(position, blocks):
        steps = jax.random.uniform(jax.random.fold_in(jax.random.fold_in(stream_key, 6), position), (blocks,), jnp.float32, least / len(shards), top_value / len(shards))
        return jnp.repeat(jnp.exp(steps), dims[position] // blocks).reshape((-1,) + (1,) * (len(dims) - position - 1))

    gain = one(*shards[0])
    for cut in shards[1:]:
        gain = gain * one(*cut)
    return gain


def noise(key, extent, scale, reach, cuts=(), held_as=jnp.bfloat16):
    factor_of = block_levels(key, extent, cuts, -0.22, 0.18) if cuts else 1.0
    array = jax.random.normal(key, extent, jnp.float32) * scale * factor_of
    return jnp.minimum(jnp.maximum(array, -reach), reach).astype(held_as)


def setup_inputs(seed: int = 0) -> dict:
    splits = jax.random.split(jax.random.key(seed), 7)
    return {
        "inputs": noise(splits[0], (MICRO, IMAGES, PIX, C), 1.0, 6.0, ((1, 32),)),
        "cotangent": noise(splits[1], (MICRO, IMAGES, PIX, C), 0.02, 0.119628906, ((1, 32),)),
        "plan": jax.random.permutation(splits[2], MICRO).astype(jnp.int32),
        "weight": noise(splits[3], (SEGMENTS, C, C), C ** -0.5, 0.109375, ((0, 4), (1, 8))),
        "squeeze": noise(splits[4], (SEGMENTS, C, R), C ** -0.5, 0.109375, ((0, 4), (1, 8))),
        "excite": noise(splits[5], (SEGMENTS, C, R), R ** -0.5, 0.3125, ((0, 4), (1, 8))),
    }


def silu_slope(value):
    sigma = jax.nn.sigmoid(value)
    return sigma * (1.0 + value * (1.0 - sigma))


def contract_rows(left, right):
    return lax.dot_general(left, right, (((0,), (0,)), ((), ())), preferred_element_type=jnp.float32)


def contract_cols(left, right):
    return lax.dot_general(left, right, (((1,), (1,)), ((), ())), preferred_element_type=jnp.float32)


def project(images, matrix):
    flat = images.reshape(-1, images.shape[-1])
    result = jnp.dot(flat, matrix, preferred_element_type=jnp.float32)
    return result.reshape(images.shape[:-1] + (matrix.shape[1],))


def forward_block(images, matrix, squeeze_w, excite_w):
    pre = project(images, matrix)
    active_map = jax.nn.silu(pre).astype(jnp.bfloat16)
    pooled = jnp.mean(active_map.astype(jnp.float32), axis=1).astype(jnp.bfloat16)
    squeezed = jnp.dot(pooled, squeeze_w, preferred_element_type=jnp.float32)
    hidden = jax.nn.silu(squeezed).astype(jnp.bfloat16)
    gate = jax.nn.sigmoid(contract_cols(hidden, excite_w))
    output = (images.astype(jnp.float32) + active_map.astype(jnp.float32) * gate[:, None, :]).astype(jnp.bfloat16)
    return output, pre, pooled, squeezed, hidden, gate


def backward_block(images, pre, squeezed, gate, upstream, matrix, squeeze_w, excite_w):
    active_map = jax.nn.silu(pre).astype(jnp.bfloat16)
    upper = upstream.astype(jnp.float32)
    d_act = upper * gate[:, None, :]
    d_gate = jnp.sum(upper * active_map.astype(jnp.float32), axis=1)
    d_excite = (d_gate * gate * (1.0 - gate)).astype(jnp.bfloat16)
    d_hidden = jnp.dot(d_excite, excite_w, preferred_element_type=jnp.float32)
    d_squeezed = (d_hidden * silu_slope(squeezed)).astype(jnp.bfloat16)
    d_pooled = contract_cols(d_squeezed, squeeze_w)
    d_act = d_act + d_pooled[:, None, :] / images.shape[1]
    d_pre = (d_act * silu_slope(pre)).astype(jnp.bfloat16)
    flat = d_pre.reshape(-1, d_pre.shape[-1])
    back = contract_cols(flat, matrix).reshape(images.shape)
    d_images = (upper + back).astype(jnp.bfloat16)
    return d_excite, d_squeezed, d_pre, d_images


def group_sum(left, right, micro, groups):
    width_l = left.shape[-1]
    width_r = right.shape[-1]
    left_g = left.reshape(micro, groups, -1, width_l).transpose(1, 0, 2, 3).reshape(groups, -1, width_l)
    right_g = right.reshape(micro, groups, -1, width_r).transpose(1, 0, 2, 3).reshape(groups, -1, width_r)

    def add_group(total, pair):
        term = contract_rows(pair[0], pair[1])
        term = lax.optimization_barrier(term.astype(jnp.bfloat16)).astype(jnp.float32)
        return total + term, None

    total, unused = lax.scan(add_group, jnp.zeros((width_l, width_r), jnp.float32), (left_g, right_g))
    return total


def reference(inputs, cotangent, plan, weight, squeeze, excite):
    ordered = inputs[plan]
    micro, images, pixels, width = ordered.shape
    groups = images // IMG_DEV
    current = ordered.reshape(micro * images, pixels, width)
    saved = []
    for segment in range(N_SEGMENT):
        output, pre, pooled, squeezed, hidden, gate = forward_block(current, weight[segment], squeeze[segment], excite[segment])
        saved.append((current, pre, pooled, squeezed, hidden, gate))
        current = output
    upstream = cotangent.reshape(micro * images, pixels, width)
    grads_w = []
    grads_s = []
    grads_e = []
    for segment in reversed(range(N_SEGMENT)):
        images_in, pre, pooled, squeezed, hidden, gate = saved[segment]
        d_excite, d_squeezed, d_pre, d_images = backward_block(images_in, pre, squeezed, gate, upstream, weight[segment], squeeze[segment], excite[segment])
        grads_w.append(group_sum(images_in, d_pre, micro, groups))
        grads_s.append(group_sum(pooled, d_squeezed, micro, groups))
        grads_e.append(group_sum(d_excite, hidden, micro, groups))
        upstream = d_images
    grads_w = grads_w[::-1]
    grads_s = grads_s[::-1]
    grads_e = grads_e[::-1]
    return (jnp.stack(grads_w), jnp.stack(grads_s), jnp.stack(grads_e))
```

```python
import functools

import jax
import jax.numpy as jnp
from jax import lax
from jax.experimental import pallas as pl
from jax.experimental.pallas import tpu as pltpu
from jax.sharding import PartitionSpec as P

MESH = pl.DeviceIdType.MESH
F32, BF16 = jnp.float32, jnp.bfloat16
STEP = 16


def round_up(value, unit):
    return -(-value // unit) * unit


def sigmoid(value):
    return jax.nn.sigmoid(value)


def silu_slope(value):
    sigma = sigmoid(value)
    return sigma * (1.0 + value * (1.0 - sigma))


def dot_nn(left, right):
    return lax.dot_general(left, right, (((1,), (0,)), ((), ())), preferred_element_type=F32)


def dot_nt(left, right):
    return lax.dot_general(left, right, (((1,), (1,)), ((), ())), preferred_element_type=F32)


def dot_tn(left, right):
    return lax.dot_general(left, right, (((0,), (0,)), ((), ())), preferred_element_type=F32)


def pipeline_kernel(
    units, sections, pixels, width, hidden,
    w_ref, x_ref, g_ref,
    h, dh, pre, act, gate, pool, sq, hid, dsq, dex,
    part, mixed, from_a, from_b, second, full, grad, work,
    sq_buf, dq_buf,
    rs_send, rs_recv, ag_send, ag_recv, sq_send, sq_recv, dq_send, dq_recv, hop_send, hop_recv,
):
    rows = h.shape[1]
    cut = round_up(rows // 2, STEP)
    top, low = pl.ds(0, cut), pl.ds(cut, rows - cut)
    seg = lax.axis_index("segment")
    me = lax.axis_index("dp")
    near_a = me + 1 - 2 * lax.rem(me, 2)
    near_b = 3 - me
    far = lax.rem(me + 2, 4)
    after = lax.rem(seg + 1, sections)
    before = lax.rem(seg + sections - 1, sections)

    barrier = pltpu.get_barrier_semaphore()
    for target in ({"dp": near_a}, {"dp": near_b}, {"dp": far}, {"segment": after}, {"segment": before}):
        pl.semaphore_signal(barrier, inc=1, device_id=target, device_id_type=MESH)
    pl.semaphore_wait(barrier, 5)

    def remote(src, dst, send, recv, target):
        return pltpu.make_async_remote_copy(
            src_ref=src, dst_ref=dst, send_sem=send, recv_sem=recv, device_id=target, device_id_type=MESH
        )

    def columns(owner):
        return pl.ds(pl.multiple_of(owner * width, width), width)

    squeeze_cols = pl.ds(4 * width, hidden)
    excite_cols = pl.ds(4 * width + hidden, hidden)

    def chunk(index):
        return pl.ds(pl.multiple_of(index * STEP, STEP), STEP)

    def images(value):
        return value.reshape(STEP // 8, 8, value.shape[-1])

    def share(buf, sends, recvs, unit, value):
        buf[unit, me] = value
        copies = [
            remote(buf.at[unit, me], buf.at[unit, me], sends.at[unit, k], recvs.at[unit, k], {"dp": peer})
            for k, peer in enumerate((near_a, near_b, far))
        ]
        for copy in copies:
            copy.start()
        for copy in copies:
            copy.wait()
        return (buf[unit, 0] + buf[unit, 1]) + (buf[unit, 2] + buf[unit, 3])

    @pl.when(seg == 0)
    def _():
        h[...] = x_ref[...]

    @pl.when(seg == sections - 1)
    def _():
        dh[...] = x_ref[...]

    def hop_forward(unit):
        return remote(work.at[unit], h.at[unit], hop_send.at[unit], hop_recv.at[unit], {"segment": after})

    def hop_backward(unit):
        return remote(
            work.at[units + unit], dh.at[unit], hop_send.at[units + unit], hop_recv.at[units + unit], {"segment": before}
        )

    def forward(unit, carry):
        @pl.when(seg > 0)
        def _():
            hop_forward(unit).wait_recv()

        def piece(slot, owner):
            part[unit, slot] = dot_nn(h[unit], w_ref[:, columns(owner)]).astype(BF16)

        def reduce_copy(k, src, dst, target):
            return remote(src, dst, rs_send.at[unit, k], rs_recv.at[unit, k], {"dp": target})

        piece(0, far)
        far_a = reduce_copy(0, part.at[unit, 0, top], from_a.at[unit, 1], near_a)
        far_b = reduce_copy(1, part.at[unit, 0, low], from_b.at[unit, 1], near_b)
        far_a.start()
        far_b.start()
        piece(1, near_a)
        own_a = reduce_copy(2, part.at[unit, 1, top], from_a.at[unit, 0], near_a)
        own_a.start()
        piece(2, near_b)
        own_b = reduce_copy(3, part.at[unit, 2, low], from_b.at[unit, 0], near_b)
        own_b.start()
        pre[unit] = dot_nn(h[unit], w_ref[:, columns(me)])

        far_a.wait_recv()

        @pl.loop(0, cut // STEP)
        def _(i):
            total = part[unit, 2, chunk(i)].astype(F32) + from_a[unit, 1, chunk(i)].astype(F32)
            mixed[unit, chunk(i)] = total.astype(BF16)

        mix_b = reduce_copy(4, mixed.at[unit, top], second.at[unit, top], near_b)
        mix_b.start()
        far_b.wait_recv()

        @pl.loop(0, (rows - cut) // STEP)
        def _(i):
            there = pl.ds(pl.multiple_of(cut + i * STEP, STEP), STEP)
            total = part[unit, 1, there].astype(F32) + from_b[unit, 1, chunk(i)].astype(F32)
            mixed[unit, there] = total.astype(BF16)

        mix_a = reduce_copy(5, mixed.at[unit, low], second.at[unit, low], near_a)
        mix_a.start()
        own_a.wait_recv()
        own_b.wait_recv()

        def finish(source, offset, i, sums):
            there = pl.ds(pl.multiple_of(offset + i * STEP, STEP), STEP)
            total = pre[unit, there] + source[unit, 0, chunk(i)].astype(F32) + second[unit, there].astype(F32)
            pre[unit, there] = total
            active = (total * sigmoid(total)).astype(BF16)
            act[unit, there] = active
            return sums + jnp.sum(images(active.astype(F32)), axis=0)

        mix_b.wait_recv()
        sums = lax.fori_loop(0, cut // STEP, functools.partial(finish, from_a, 0), jnp.zeros((8, width), F32))
        mix_a.wait_recv()
        sums = lax.fori_loop(0, (rows - cut) // STEP, functools.partial(finish, from_b, cut), sums)
        pooled = (sums / pixels).astype(BF16)
        pool[unit] = pooled.astype(F32)
        squeezed = share(sq_buf, sq_send, sq_recv, unit, dot_nn(pooled, w_ref[:, squeeze_cols]))
        hidden_now = (squeezed * sigmoid(squeezed)).astype(BF16)
        sq[unit] = squeezed
        hid[unit] = hidden_now.astype(F32)
        gates = sigmoid(dot_nt(hidden_now, w_ref[:, excite_cols]))
        gate[unit] = gates

        @pl.when(seg < sections - 1)
        def _():
            @pl.loop(0, rows // STEP)
            def _(i):
                scaled = images(act[unit, chunk(i)].astype(F32)) * gates
                total = h[unit, chunk(i)].astype(F32) + scaled.reshape(STEP, width)
                work[unit, chunk(i)] = total.astype(BF16)

            hop_forward(unit).start()

        for copy in (far_a, far_b, own_a, own_b, mix_b, mix_a):
            copy.wait_send()
        return carry

    lax.fori_loop(0, units, forward, 0)

    grad[...] = jnp.zeros_like(grad)

    def backward(unit, carry):
        @pl.when(seg < sections - 1)
        def _():
            hop_backward(unit).wait_recv()

        def weigh(i, sums):
            product = dh[unit, chunk(i)].astype(F32) * act[unit, chunk(i)].astype(F32)
            return sums + jnp.sum(images(product), axis=0)

        d_gate = lax.fori_loop(0, rows // STEP, weigh, jnp.zeros((8, width), F32))
        gates = gate[unit]
        d_excite = (d_gate * gates * (1.0 - gates)).astype(BF16)
        dex[unit] = d_excite.astype(F32)
        d_hidden = share(dq_buf, dq_send, dq_recv, unit, dot_nn(d_excite, w_ref[:, excite_cols]))
        d_squeezed = (d_hidden * silu_slope(sq[unit])).astype(BF16)
        dsq[unit] = d_squeezed.astype(F32)
        d_pool = dot_nt(d_squeezed, w_ref[:, squeeze_cols]) / pixels

        @pl.loop(0, rows // STEP)
        def _(i):
            d_act = images(dh[unit, chunk(i)].astype(F32)) * gates + d_pool
            d_pre = d_act * silu_slope(images(pre[unit, chunk(i)]))
            full[unit, 0, chunk(i)] = d_pre.reshape(STEP, width).astype(BF16)

        def gather_copy(k, src, dst, target):
            return remote(src, dst, ag_send.at[unit, k], ag_recv.at[unit, k], {"dp": target})

        own_a = gather_copy(0, full.at[unit, 0], full.at[unit, 1], near_a)
        own_b = gather_copy(1, full.at[unit, 0], full.at[unit, 2], near_b)
        pass_b = gather_copy(2, full.at[unit, 1, top], full.at[unit, 3, top], near_b)
        pass_a = gather_copy(3, full.at[unit, 2, low], full.at[unit, 3, low], near_a)
        own_a.start()
        own_b.start()

        def back(slot, owner):
            return dot_nt(full[unit, slot], w_ref[:, columns(owner)])

        @pl.when(seg > 0)
        def _():
            pre[unit] = back(0, me) + dh[unit].astype(F32)

        own_a.wait_recv()
        pass_b.start()
        own_b.wait_recv()
        pass_a.start()

        @pl.when(seg > 0)
        def _():
            pre[unit] += back(1, near_a)
            pre[unit] += back(2, near_b)

        pass_b.wait_recv()
        pass_a.wait_recv()

        @pl.when(seg > 0)
        def _():
            work[units + unit] = (pre[unit] + back(3, far)).astype(BF16)
            hop_backward(unit).start()

        for slot in range(4):
            grad[slot] += dot_tn(h[unit], full[unit, slot])
        for copy in (own_a, own_b, pass_b, pass_a):
            copy.wait_send()
        return carry

    lax.fori_loop(0, units, backward, 0)

    for slot, owner in enumerate((me, near_a, near_b, far)):
        g_ref[:, columns(owner)] = grad[slot].astype(BF16)

    def stacked(ref):
        return ref[...].reshape(units * 8, ref.shape[-1]).astype(BF16)

    g_ref[:, squeeze_cols] = dot_tn(stacked(pool), stacked(dsq)).astype(BF16)
    g_ref[:, excite_cols] = dot_tn(stacked(dex), stacked(hid)).astype(BF16)

    @pl.when(seg < sections - 1)
    def _():
        for unit in range(units):
            hop_forward(unit).wait_send()

    @pl.when(seg > 0)
    def _():
        for unit in range(units):
            hop_backward(unit).wait_send()


def run_pipeline(weights, x, sections, pixels, hidden):
    units, rows, width = x.shape
    cut = round_up(rows // 2, STEP)
    vmem, dma = pltpu.VMEM, pltpu.SemaphoreType.DMA
    return pl.pallas_call(
        functools.partial(pipeline_kernel, units, sections, pixels, width, hidden),
        out_shape=jax.ShapeDtypeStruct(weights.shape, BF16),
        in_specs=[pl.BlockSpec(memory_space=pltpu.VMEM)] * 2,
        out_specs=pl.BlockSpec(memory_space=pltpu.VMEM),
        scratch_shapes=[
            vmem((units, rows, width), BF16),
            vmem((units, rows, width), BF16),
            vmem((units, rows, width), F32),
            vmem((units, rows, width), BF16),
            vmem((units, 8, width), F32),
            vmem((units, 8, width), F32),
            vmem((units, 8, hidden), F32),
            vmem((units, 8, hidden), F32),
            vmem((units, 8, hidden), F32),
            vmem((units, 8, width), F32),
            vmem((units, 3, rows, width), BF16),
            vmem((units, rows, width), BF16),
            vmem((units, 2, cut, width), BF16),
            vmem((units, 2, rows - cut, width), BF16),
            vmem((units, rows, width), BF16),
            vmem((units, 4, rows, width), BF16),
            vmem((4, width, width), F32),
            vmem((2 * units, rows, width), BF16),
            vmem((units, 4, 8, hidden), F32),
            vmem((units, 4, 8, hidden), F32),
            dma((units, 6)), dma((units, 6)),
            dma((units, 4)), dma((units, 4)),
            dma((units, 3)), dma((units, 3)),
            dma((units, 3)), dma((units, 3)),
            dma((2 * units,)), dma((2 * units,)),
        ],
        compiler_params=pltpu.CompilerParams(
            collective_id=0, has_side_effects=True, vmem_limit_bytes=67_000_000
        ),
        name="pipeline",
    )(weights, x)


def spread(value, parts, sets, piece, run):
    lead = value.shape[:-1]
    split = value.reshape(lead + (parts, sets, piece))
    split = jnp.pad(split, [(0, 0)] * (len(lead) + 2) + [(0, run - piece)])
    return jnp.swapaxes(split, -3, -2).reshape(lead + (sets, parts * run))


def gathered(value, parts, sets, piece, run):
    lead = value.shape[:-1]
    split = jnp.swapaxes(value.reshape(lead + (sets, parts, run)), -3, -2)[..., :piece]
    return split.reshape(lead + (parts * sets * piece,))


def on_device(inputs, cotangent, plan, weight, squeeze, excite):
    sections, parts, sets = (lax.axis_size(name) for name in ("segment", "fsdp", "dp"))
    units, each, pixels, channels = inputs.shape
    piece = channels // (parts * sets)
    run = round_up(piece, 16)
    hidden_real = squeeze.shape[-1]
    hidden = round_up(hidden_real, 128)
    me = lax.axis_index("dp")

    def rows_of(array):
        return lax.dynamic_slice_in_dim(array[0], me * piece, piece, axis=0)

    own_w = spread(rows_of(weight), parts, sets, piece, run).reshape(piece, -1)
    own = jnp.concatenate(
        [
            own_w,
            jnp.pad(rows_of(squeeze), ((0, 0), (0, hidden - hidden_real))),
            jnp.pad(rows_of(excite), ((0, 0), (0, hidden - hidden_real))),
        ],
        axis=1,
    )
    own = jnp.pad(own, ((0, run - piece), (0, 0)))
    weights = lax.all_gather(own, "fsdp", axis=0, tiled=True)

    last = lax.axis_index("segment") == sections - 1
    x = jnp.where(last, cotangent, inputs[plan])
    x = spread(x, parts, sets, piece, run)
    x = lax.all_to_all(x, "dp", split_axis=3, concat_axis=0, tiled=False)
    x = x.transpose(1, 3, 0, 2, 4)
    x = jnp.pad(x, ((0, 0), (0, pixels % 2), (0, 0), (0, 0), (0, 0)))
    x = x.reshape(units, -1, x.shape[-1])

    grads = run_pipeline(weights, x, sections, pixels, hidden)
    mine = lax.psum_scatter(grads, "fsdp", scatter_dimension=0, tiled=True)[:piece]
    width = parts * run
    grad_w = gathered(mine[:, : sets * width].astype(F32), parts, sets, piece, run)
    grad_s = mine[:, sets * width :][:, :hidden_real].astype(F32)
    grad_e = mine[:, sets * width + hidden :][:, :hidden_real].astype(F32)
    return (grad_w[None], grad_s[None], grad_e[None])


def solution(mesh):
    data = P(None, ("fsdp", "dp"), None, None)
    owned = P("segment", "fsdp", None)
    result = P("segment", ("fsdp", "dp"), None)
    return jax.shard_map(
        on_device,
        mesh=mesh,
        in_specs=(data, data, P(), owned, owned, owned),
        out_specs=(result,) * 3,
        check_vma=False,
    )
```
